32 devices in a mesh: grp: 1, wide: 8 (over z, y), narrow: 4 (over x, core).
Axes of the slice: x: 2, y: 2, z: 4, core: 2. Of those that a mesh axis runs over, the one named last changes fastest.
Arguments:
- vectors: bfloat16 [512, 2, 3, 16, 512], P('grp', None, None, 'wide', 'narrow'), may hold values from -6 to 6
- links: float32 [3, 2, 3, 3, 16, 512], P('grp', None, None, None, 'wide', 'narrow'), may hold values from -4 to 4
- directions: int32 [3], replicated, may hold values from 0 to 2, each once
- peram: bfloat16 [2, 512, 256], P('grp', 'wide', 'narrow'), may hold values from -0.1875 to 0.1875
Outputs:
- elementals: float32 [3, 2, 512, 512], P('grp', None, 'wide')
- products: float32 [3, 2, 512, 256], P('grp', None, 'wide', 'narrow')
The draws below stay inside these ranges and needn't reach their ends.
All inputs are finite; a program needn't handle non-finite values.
Results may differ from the reference program's by a relative error of at most 0.004.
Values may be sent and summed in bfloat16 or wider, within the bound.
A program may use at most 64 MiB of HBM per device.

```python
import math
import jax
import jax.numpy as jnp
from jax import lax

NVEC = 512
NCOL = 256
NDIR = 3
NX = 16
NY = 32
NZ = 16


def level_of(key, dims, pieces, least, largest):
    gain = 1.0
    for dim, parts in pieces:
        draws = jax.random.uniform(jax.random.fold_in(jax.random.fold_in(key, 6), dim), (parts,), jnp.float32, least / len(pieces), largest / len(pieces))
        gain = gain * jnp.repeat(jnp.exp(draws), dims[dim] // parts).reshape((-1,) + (1,) * (len(dims) - 1 - dim))
    return gain


def centred(key, dims, deviation, bound, shards=(), held_as=jnp.bfloat16):
    result = deviation * jax.random.normal(key, dims, jnp.float32)
    if shards:
        result = result * level_of(key, dims, shards, -0.22, 0.18)
    return jnp.clip(result, -bound, bound).astype(held_as)


def setup_inputs(seed: int = 0, part: int = 0) -> dict:
    streams_of = jax.random.split(jax.random.key(seed), 5)
    part_keys = jax.random.split(jax.random.fold_in(streams_of[4], part), 5)
    return {
        "vectors": centred(part_keys[0], (NVEC, 2, 3, NX, NY * NZ), 1.0, 6.0, ((3, 8), (4, 4))),
        "links": centred(part_keys[1], (3, 2, 3, 3, NX, NY * NZ), 0.577, 4.0, ((4, 8), (5, 4)), jnp.float32),
        "directions": jax.random.permutation(streams_of[2], NDIR).astype(jnp.int32),
        "peram": centred(part_keys[3], (2, NVEC, NCOL), (2 * NVEC) ** -0.5, 0.1875, ((1, 8), (2, 4))),
    }


def covariant_product(link_field, shifted):
    link_real = link_field[0][None]
    link_imag = link_field[1][None]
    vec_real = shifted[:, 0][:, None]
    vec_imag = shifted[:, 1][:, None]
    out_real = lax.optimization_barrier(jnp.sum(link_real * vec_real - link_imag * vec_imag, axis=2))
    out_imag = lax.optimization_barrier(jnp.sum(link_real * vec_imag + link_imag * vec_real, axis=2))
    return jnp.stack([out_real, out_imag], 1).astype(jnp.bfloat16)

def reference(vectors, links, directions, peram):
    vec_count = vectors.shape[0]
    col_count = peram.shape[2]
    norm_factor = 1.0 / math.sqrt(12.0 * NX * NY * NZ)

    def plane_step(carry, position):
        plane = lax.dynamic_index_in_dim(vectors, position, 3, keepdims=False)
        ahead = lax.dynamic_index_in_dim(vectors, (position + 1) % NX, 3, keepdims=False)
        link_plane = lax.dynamic_index_in_dim(links, position, 4, keepdims=False)
        along_second = jnp.roll(plane, -NZ, axis=3)
        along_third = jnp.roll(plane.reshape(vec_count, 2, 3, NY, NZ), -1, axis=4).reshape(plane.shape)
        rotated = jnp.concatenate([-plane[:, 1:2], plane[:, 0:1]], 1)
        left_block = jnp.concatenate([plane.reshape(vec_count, -1), rotated.reshape(vec_count, -1)], 0)
        partials = []
        for slot_index in range(NDIR):
            chosen = directions[slot_index]
            shifted = jnp.where(chosen == 0, ahead, jnp.where(chosen == 1, along_second, along_third))
            link_field = jnp.where(chosen == 0, link_plane[0], jnp.where(chosen == 1, link_plane[1], link_plane[2]))
            product = covariant_product(link_field, shifted).reshape(vec_count, -1)
            partials.append(jnp.dot(left_block, product.T, preferred_element_type=jnp.float32))
        return (carry + jnp.stack(partials), None)
    initial = jnp.zeros((NDIR, 2 * vec_count, vec_count), jnp.float32)
    total, _ = lax.scan(plane_step, initial, jnp.arange(NX, dtype=jnp.int32))
    halves = total.reshape(NDIR, 2, vec_count, vec_count) * norm_factor
    real_part = halves[:, 0]
    imag_part = halves[:, 1]
    elementals = jnp.stack([real_part - jnp.swapaxes(real_part, 1, 2), imag_part + jnp.swapaxes(imag_part, 1, 2)], 1)
    elem_low = elementals.astype(jnp.bfloat16)
    left_rows = jnp.concatenate([elem_low[:, 0], elem_low[:, 1]], 2).reshape(NDIR * vec_count, 2 * vec_count)
    peram_real = peram[0]
    peram_imag = peram[1]
    right_block = jnp.concatenate([jnp.concatenate([peram_real, peram_imag], 1), jnp.concatenate([-peram_imag, peram_real], 1)], 0)
    summed = jnp.dot(left_rows, right_block, preferred_element_type=jnp.float32)
    products = summed.reshape(NDIR, vec_count, 2, col_count).transpose(0, 2, 1, 3)
    return (elementals, products)
```

```python
import functools
import math

import jax
import jax.numpy as jnp
from jax import lax
from jax.experimental import pallas as pl
from jax.experimental.pallas import tpu as pltpu
from jax.sharding import PartitionSpec as P

LZ = 16
ORDER = (2, 1, 0)
CHUNK = 32
MESH = pl.DeviceIdType.MESH
NT = (((1,), (1,)), ((), ()))


def kernel(wides, narrows, norm, vec, links, dirs, peram, elem_out, prod_out,
           pack, halo0, halo1, f_re, f_im, half, part, got_core, got_row, got_wide,
           thin, full, prods, per_all,
           h_send, h_recv, p_send, p_recv, c_send, c_recv, r_send, r_recv,
           w_send, w_recv, g_send, g_recv):
    planes, comps, count, lanes = vec.shape
    groups = lanes // LZ
    per_group = count // groups
    rows = count // wides
    share = 2 * rows // narrows
    across = narrows // 2
    me_w = lax.axis_index("wide")
    me_n = lax.axis_index("narrow")
    core = lax.rem(me_n, 2)
    me_x = me_n // 2

    def at_wide(step):
        return {"wide": lax.rem(me_w + step, wides)}

    def at_narrow(step):
        return {"narrow": lax.rem(me_n + step, narrows)}

    def at_row(step):
        return {"narrow": lax.rem(me_x + step, across) * 2 + core}

    def copy(src, dst, send, recv, where):
        return pltpu.make_async_remote_copy(
            src_ref=src, dst_ref=dst, send_sem=send, recv_sem=recv,
            device_id=where, device_id_type=MESH)

    barrier = pltpu.get_barrier_semaphore()
    for step in range(1, wides):
        pl.semaphore_signal(barrier, inc=1, device_id=at_wide(step), device_id_type=MESH)
    for step in range(1, narrows):
        pl.semaphore_signal(barrier, inc=1, device_id=at_narrow(step), device_id_type=MESH)

    lane = lax.broadcasted_iota(jnp.int32, (CHUNK, lanes), 1)

    def pack_rows(i, carry):
        slab = i // (per_group // CHUNK)
        start = pl.multiple_of(lax.rem(i, per_group // CHUNK) * CHUNK, CHUNK)
        plane = slab // comps
        comp = lax.rem(slab, comps)
        total = jnp.zeros((CHUNK, lanes), jnp.float32)
        for group in range(groups):
            piece = vec[plane, comp, pl.ds(group * per_group + start, CHUNK), :].astype(jnp.float32)
            if group:
                piece = pltpu.roll(piece, group * LZ, 1)
            total = jnp.where(lane // LZ == group, piece, total)
        pack[plane, comp, pl.ds(start, CHUNK), :] = total.astype(jnp.bfloat16)
        return carry

    lax.fori_loop(0, planes * comps * (per_group // CHUNK), pack_rows, 0)

    pl.semaphore_wait(barrier, wides + narrows - 2)
    first_copy = copy(vec.at[0], halo0, h_send.at[0], h_recv.at[0], at_wide(wides - 1))
    second_copy = copy(pack, halo1, h_send.at[1], h_recv.at[1], at_narrow(narrows - 1))
    second_copy.start()
    first_copy.start()
    per_copies = [
        copy(peram, per_all.at[me_w], p_send.at[step - 1], p_recv.at[step - 1], at_wide(step))
        for step in range(1, wides)
    ]
    for one in per_copies:
        one.start()
    per_all[me_w] = peram[...]

    def shifted(direction, plane, comp, start):
        here = pl.ds(start, CHUNK)
        if direction == 0:
            if plane + 1 < planes:
                return vec[plane + 1, comp, here, :].astype(jnp.float32)
            return halo0[comp, here, :].astype(jnp.float32)
        own = vec[plane, comp, here, :].astype(jnp.float32)
        if direction == 1:
            group = start // per_group
            inside = pl.multiple_of(lax.rem(start, per_group), CHUNK)
            ahead = halo1[plane, comp, pl.ds(inside, CHUNK), :].astype(jnp.float32)
            ahead = pltpu.roll(ahead, lanes - LZ - LZ * group, 1)
            return jnp.where(lane < lanes - LZ, pltpu.roll(own, lanes - LZ, 1), ahead)
        return jnp.where(
            lax.rem(lane, LZ) < LZ - 1, pltpu.roll(own, lanes - 1, 1), pltpu.roll(own, LZ - 1, 1))

    def forward(direction):
        for plane in range(planes):
            def chunk(i, carry):
                start = pl.multiple_of(i * CHUNK, CHUNK)
                values = [shifted(direction, plane, comp, start) for comp in range(comps)]
                for a in range(3):
                    real = imag = None
                    for b in range(3):
                        link_r = links[direction, 0, a, b, plane:plane + 1, :]
                        link_i = links[direction, 1, a, b, plane:plane + 1, :]
                        term_r = link_r * values[b] - link_i * values[3 + b]
                        term_i = link_r * values[3 + b] + link_i * values[b]
                        real = term_r if real is None else real + term_r
                        imag = term_i if imag is None else imag + term_i
                    real = real.astype(jnp.bfloat16)
                    imag = imag.astype(jnp.bfloat16)
                    low = (plane * comps + a) * lanes
                    high = low + 3 * lanes
                    f_re[pl.ds(start, CHUNK), low:low + lanes] = real
                    f_re[pl.ds(start, CHUNK), high:high + lanes] = imag
                    f_im[pl.ds(start, CHUNK), low:low + lanes] = imag
                    f_im[pl.ds(start, CHUNK), high:high + lanes] = -real
                return carry

            lax.fori_loop(0, count // CHUNK, chunk, 0)

    def compute(direction):
        forward(direction)
        left = jnp.concatenate(
            [vec[plane, comp] for plane in range(planes) for comp in range(comps)], 1)
        half[0] = lax.dot_general(left, f_re[...], NT, preferred_element_type=jnp.float32)
        half[1] = lax.dot_general(left, f_im[...], NT, preferred_element_type=jnp.float32)
        block = lanes
        for c in range(2):
            for top in range(0, count, block):
                turned = half[c, :, top:top + block].T
                own = half[c, top:top + block, :]
                terms = ((own - turned) if c == 0 else (own + turned)) * norm
                for low in range(0, block, share):
                    row = top + low
                    owner = c * across + (row % rows) // share
                    part[direction, owner % 2, owner // 2, row // rows] = (
                        terms[low:low + share].astype(jnp.bfloat16))

    def core_copy(d):
        return copy(part.at[d, 1 - core], got_core.at[d], c_send.at[d], c_recv.at[d],
                    {"narrow": me_x * 2 + 1 - core})

    def row_copy(d, step):
        return copy(part.at[d, core, lax.rem(me_x + step, across)], got_row.at[d, step - 1],
                    r_send.at[d, step - 1], r_recv.at[d, step - 1], at_row(step))

    def wide_copy(d, step):
        return copy(part.at[d, core, me_x, lax.rem(me_w + step, wides)],
                    got_wide.at[d, step - 1],
                    w_send.at[d, step - 1], w_recv.at[d, step - 1], at_wide(step))

    def full_copy(d, step):
        return copy(thin.at[d], full.at[d, me_n], g_send.at[d, step - 1], g_recv.at[d, step - 1],
                    at_narrow(step))

    def core_done(d):
        core_copy(d).wait()
        for x in range(across):
            def add(w, carry):
                part[d, core, x, w] = (
                    part[d, core, x, w].astype(jnp.float32)
                    + got_core[d, x, w].astype(jnp.float32)).astype(jnp.bfloat16)
                return carry
            lax.fori_loop(0, wides, add, 0)
        for step in range(1, across):
            row_copy(d, step).start()

    def row_done(d):
        for step in range(1, across):
            row_copy(d, step).wait()

        def add(w, carry):
            total = part[d, core, me_x, w].astype(jnp.float32)
            for step in range(1, across):
                total = total + got_row[d, step - 1, w].astype(jnp.float32)
            part[d, core, me_x, w] = total.astype(jnp.bfloat16)
            return carry

        lax.fori_loop(0, wides, add, 0)
        for step in range(1, wides):
            wide_copy(d, step).start()

    def wide_done(d):
        for step in range(1, wides):
            wide_copy(d, step).wait()
        total = part[d, core, me_x, me_w].astype(jnp.float32)
        for step in range(1, wides):
            total = total + got_wide[d, step - 1].astype(jnp.float32)
        total = total.astype(jnp.bfloat16)
        thin[d] = total
        full[d, me_n] = total
        for step in range(1, narrows):
            full_copy(d, step).start()

    def finish(d):
        for step in range(1, narrows):
            full_copy(d, step).wait()
        real = full[d, 0:across].astype(jnp.float32).reshape(rows, count).astype(jnp.bfloat16)
        imag = full[d, across:narrows].astype(jnp.float32).reshape(rows, count).astype(jnp.bfloat16)
        per_r = per_all[:, 0].reshape(count, per_all.shape[3])
        per_i = per_all[:, 1].reshape(count, per_all.shape[3])

        def times(x, y):
            return jnp.dot(x, y, preferred_element_type=jnp.float32)

        prods[d, 0] = times(real, per_r) - times(imag, per_i)
        prods[d, 1] = times(real, per_i) + times(imag, per_r)

    compute(2)
    core_copy(2).start()
    second_copy.wait()
    compute(1)
    core_copy(1).start()
    core_done(2)
    first_copy.wait()
    compute(0)
    core_copy(0).start()
    row_done(2)
    core_done(1)
    core_done(0)
    row_done(1)
    wide_done(2)
    row_done(0)
    for one in per_copies:
        one.wait()
    wide_done(1)
    finish(2)
    wide_done(0)
    finish(1)
    finish(0)
    for slot in range(3):
        d = dirs[slot]
        elem_out[slot] = full[d].astype(jnp.float32).reshape(2, rows, count)
        prod_out[slot] = prods[d]


def on_device(vectors, links, directions, peram):
    count, _, _, planes, lanes = vectors.shape
    wides = lax.axis_size("wide")
    narrows = lax.axis_size("narrow")
    slots = directions.shape[0]
    cols = peram.shape[2]
    rows = count // wides
    share = 2 * rows // narrows
    across = narrows // 2
    norm = 1.0 / math.sqrt(12.0 * planes * wides * lanes * narrows)
    turned = vectors.transpose(3, 1, 2, 0, 4).reshape(planes, 6, count, lanes)
    vmem = pl.BlockSpec(memory_space=pltpu.VMEM)
    low = jnp.bfloat16
    dma = pltpu.SemaphoreType.DMA
    return pl.pallas_call(
        functools.partial(kernel, wides, narrows, norm),
        out_shape=(
            jax.ShapeDtypeStruct((slots, 2, rows, count), jnp.float32),
            jax.ShapeDtypeStruct((slots, 2, rows, cols), jnp.float32),
        ),
        in_specs=[vmem, vmem, pl.BlockSpec(memory_space=pltpu.SMEM), vmem],
        out_specs=(vmem, vmem),
        scratch_shapes=[
            pltpu.VMEM((planes, 6, count * LZ // lanes, lanes), low),
            pltpu.VMEM((6, count, lanes), low),
            pltpu.VMEM((planes, 6, count * LZ // lanes, lanes), low),
            pltpu.VMEM((count, planes * 6 * lanes), low),
            pltpu.VMEM((count, planes * 6 * lanes), low),
            pltpu.VMEM((2, count, count), jnp.float32),
            pltpu.VMEM((3, 2, across, wides, share, count), low),
            pltpu.VMEM((3, across, wides, share, count), low),
            pltpu.VMEM((3, across - 1, wides, share, count), low),
            pltpu.VMEM((3, wides - 1, share, count), low),
            pltpu.VMEM((3, share, count), low),
            pltpu.VMEM((3, narrows, share, count), low),
            pltpu.VMEM((3, 2, rows, cols), jnp.float32),
            pltpu.VMEM((wides, 2, rows, cols), low),
            dma((2,)), dma((2,)),
            dma((wides - 1,)), dma((wides - 1,)),
            dma((3,)), dma((3,)),
            dma((3, across - 1)), dma((3, across - 1)),
            dma((3, wides - 1)), dma((3, wides - 1)),
            dma((3, narrows - 1)), dma((3, narrows - 1)),
        ],
        compiler_params=pltpu.CompilerParams(
            collective_id=0, has_side_effects=True, vmem_limit_bytes=50 * 2**20),
    )(turned, links, directions, peram)


def solution(mesh):
    placed = (
        P("grp", None, None, "wide", "narrow"),
        P("grp", None, None, None, "wide", "narrow"),
        P(),
        P("grp", "wide", "narrow"),
    )
    return jax.shard_map(
        on_device,
        mesh=mesh,
        in_specs=placed,
        out_specs=(P("grp", None, "wide", None), P("grp", None, "wide", "narrow")),
        check_vma=False,
    )
```

```python
import functools
import math

import jax
import jax.numpy as jnp
from jax import lax
from jax.experimental import pallas as pl
from jax.experimental.pallas import tpu as pltpu
from jax.sharding import PartitionSpec as P

LZ = 16
PIECES = 4
CHUNK = 32
MESH = pl.DeviceIdType.MESH
NT = (((1,), (1,)), ((), ()))


def kernel(wides, narrows, norm, vec, links, dirs, peram, elem_out, prod_out,
           pack, halo0, halo1, f_re, f_im, half, keep, part, got_core, got_row, got_wide,
           got_all, thin, full, prods, per_all,
           h_send, h_recv, s_send, s_recv, p_send, p_recv, c_send, c_recv, r_send, r_recv,
           w_send, w_recv, a_send, a_recv, g_send, g_recv):
    planes, comps, count, lanes = vec.shape
    groups = lanes // LZ
    per_group = count // groups
    rows = count // wides
    share = 2 * rows // narrows
    across = narrows // 2
    me_w = lax.axis_index("wide")
    me_n = lax.axis_index("narrow")
    core = lax.rem(me_n, 2)
    me_x = me_n // 2

    def at_wide(step):
        return {"wide": lax.rem(me_w + step, wides)}

    def at_narrow(step):
        return {"narrow": lax.rem(me_n + step, narrows)}

    def at_chip(x, step):
        return {"wide": lax.rem(me_w + step, wides), "narrow": x * 2 + core}

    def copy(src, dst, send, recv, where):
        return pltpu.make_async_remote_copy(
            src_ref=src, dst_ref=dst, send_sem=send, recv_sem=recv,
            device_id=where, device_id_type=MESH)

    barrier = pltpu.get_barrier_semaphore()

    def greet(where):
        pl.semaphore_signal(barrier, inc=1, device_id=where, device_id_type=MESH)

    for x_step in range(across):
        for w_step in range(wides):
            if x_step or w_step:
                greet(at_chip(lax.rem(me_x + x_step, across), w_step))
        greet({"narrow": lax.rem(me_x + x_step, across) * 2 + 1 - core})

    lane = lax.broadcasted_iota(jnp.int32, (CHUNK, lanes), 1)

    pl.semaphore_wait(barrier, across * wides - 1 + across)
    pieces = h_send.shape[0]
    depth = count // pieces
    halo_copies = [
        copy(vec.at[0, :, pl.ds(piece * depth, depth)], halo0.at[:, pl.ds(piece * depth, depth)],
             h_send.at[piece], h_recv.at[piece], at_wide(wides - 1))
        for piece in range(pieces)
    ]
    for one in halo_copies:
        one.start()

    def pack_rows(i, carry):
        slab = i // (per_group // CHUNK)
        start = pl.multiple_of(lax.rem(i, per_group // CHUNK) * CHUNK, CHUNK)
        plane = slab // comps
        comp = lax.rem(slab, comps)
        total = jnp.zeros((CHUNK, lanes), jnp.float32)
        for group in range(groups):
            piece = vec[plane, comp, pl.ds(group * per_group + start, CHUNK), :].astype(jnp.float32)
            if group:
                piece = pltpu.roll(piece, group * LZ, 1)
            total = jnp.where(lane // LZ == group, piece, total)
        pack[plane, comp, pl.ds(start, CHUNK), :] = total.astype(jnp.bfloat16)
        return carry

    lax.fori_loop(0, planes * comps * (per_group // CHUNK), pack_rows, 0)
    second_copy = copy(pack, halo1, s_send.at[0], s_recv.at[0], at_narrow(narrows - 1))
    second_copy.start()
    per_copies = [
        copy(peram, per_all.at[me_w], p_send.at[step - 1], p_recv.at[step - 1], at_wide(step))
        for step in range(1, wides)
    ]
    for one in per_copies:
        one.start()
    per_all[me_w] = peram[...]

    def shifted(direction, plane, comp, start):
        here = pl.ds(start, CHUNK)
        if direction == 0:
            if plane + 1 < planes:
                return vec[plane + 1, comp, here, :].astype(jnp.float32)
            return halo0[comp, here, :].astype(jnp.float32)
        own = vec[plane, comp, here, :].astype(jnp.float32)
        if direction == 1:
            group = start // per_group
            inside = pl.multiple_of(lax.rem(start, per_group), CHUNK)
            ahead = halo1[plane, comp, pl.ds(inside, CHUNK), :].astype(jnp.float32)
            ahead = pltpu.roll(ahead, lanes - LZ - LZ * group, 1)
            return jnp.where(lane < lanes - LZ, pltpu.roll(own, lanes - LZ, 1), ahead)
        return jnp.where(
            lax.rem(lane, LZ) < LZ - 1, pltpu.roll(own, lanes - 1, 1), pltpu.roll(own, LZ - 1, 1))

    def forward(direction, planes_here, first=0, last=count):
        for plane in planes_here:
            def chunk(i, carry):
                start = pl.multiple_of(i * CHUNK, CHUNK)
                values = [shifted(direction, plane, comp, start) for comp in range(comps)]
                for a in range(3):
                    real = imag = None
                    for b in range(3):
                        link_r = links[direction, 0, a, b, plane:plane + 1, :]
                        link_i = links[direction, 1, a, b, plane:plane + 1, :]
                        term_r = link_r * values[b] - link_i * values[3 + b]
                        term_i = link_r * values[3 + b] + link_i * values[b]
                        real = term_r if real is None else real + term_r
                        imag = term_i if imag is None else imag + term_i
                    real = real.astype(jnp.bfloat16)
                    imag = imag.astype(jnp.bfloat16)
                    low = (plane * comps + a) * lanes
                    high = low + 3 * lanes
                    f_re[pl.ds(start, CHUNK), low:low + lanes] = real
                    f_re[pl.ds(start, CHUNK), high:high + lanes] = imag
                    f_im[pl.ds(start, CHUNK), low:low + lanes] = imag
                    f_im[pl.ds(start, CHUNK), high:high + lanes] = -real
                return carry

            lax.fori_loop(first // CHUNK, last // CHUNK, chunk, 0)

    mid = count // 2
    xs_of = (range(0, across // 2), range(across // 2, across))

    def multiply(c, low, high):
        left = jnp.concatenate(
            [vec[plane, comp] for plane in range(planes) for comp in range(comps)], 1)
        right = f_re if c == 0 else f_im
        half[c, :, low:high] = lax.dot_general(
            left, right[low:high, :], NT, preferred_element_type=jnp.float32)

    def core_copy(d, c):
        xs = pl.ds(xs_of[c][0], len(xs_of[c]))
        return copy(keep.at[d, 1 - core, xs], got_core.at[d, xs], c_send.at[d, c],
                    c_recv.at[d, c], {"narrow": me_x * 2 + 1 - core})

    def balance(d, c):
        block = lanes
        for top in range(0, count, block):
            turned = half[c, :, top:top + block].T
            own = half[c, top:top + block, :]
            terms = ((own - turned) if c == 0 else (own + turned)) * norm
            for low in range(0, block, share):
                row = top + low
                owner = c * across + (row % rows) // share
                keep[d, owner % 2, owner // 2, row // rows] = terms[low:low + share]
        core_copy(d, c).start()

    def row_copy(d, x, step):
        return copy(part.at[d, x], got_row.at[d - 1, step - 1],
                    r_send.at[d - 1, step - 1], r_recv.at[d - 1, step - 1], at_chip(x, 0))

    def wide_copy(d, step):
        return copy(part.at[d, me_x, lax.rem(me_w + step, wides)],
                    got_wide.at[d - 1, step - 1],
                    w_send.at[d - 1, step - 1], w_recv.at[d - 1, step - 1], at_wide(step))

    def chip_copy(x, x_step, w_step):
        return copy(part.at[0, x, lax.rem(me_w + w_step, wides)], got_all.at[x_step, w_step],
                    a_send.at[x_step, w_step], a_recv.at[x_step, w_step], at_chip(x, w_step))

    def full_copy(d, step):
        return copy(thin.at[d], full.at[d, me_n], g_send.at[d, step - 1], g_recv.at[d, step - 1],
                    at_narrow(step))

    def push(d, c):
        core_copy(d, c).wait()
        for x in xs_of[c]:
            def add(w, carry):
                total = keep[d, core, x, w] + got_core[d, x, w]
                keep[d, core, x, w] = total
                part[d, x, w] = total.astype(jnp.bfloat16)
                return carry

            lax.fori_loop(0, wides, add, 0)
            x_step = lax.rem(x - me_x + across, across)
            if d:
                @pl.when(x_step > 0)
                def _():
                    row_copy(d, x, x_step).start()
            else:
                for w_step in range(1, wides):
                    chip_copy(x, x_step, w_step).start()

                @pl.when(x_step > 0)
                def _():
                    chip_copy(x, x_step, 0).start()

    def row_done(d):
        for step in range(1, across):
            row_copy(d, lax.rem(me_x + step, across), step).wait()

        def add(w, carry):
            total = keep[d, core, me_x, w]
            for step in range(1, across):
                total = total + got_row[d - 1, step - 1, w].astype(jnp.float32)
            keep[d, core, me_x, w] = total
            part[d, me_x, w] = total.astype(jnp.bfloat16)
            return carry

        lax.fori_loop(0, wides, add, 0)
        for step in range(1, wides):
            wide_copy(d, step).start()

    def total_done(d):
        total = keep[d, core, me_x, me_w]
        if d:
            for step in range(1, wides):
                wide_copy(d, step).wait()
            for step in range(1, wides):
                total = total + got_wide[d - 1, step - 1].astype(jnp.float32)
        else:
            steps = [(x, w) for x in range(across) for w in range(wides) if x or w]
            for x_step, w_step in steps:
                chip_copy(lax.rem(me_x + x_step, across), x_step, w_step).wait()
            for x_step, w_step in steps:
                total = total + got_all[x_step, w_step].astype(jnp.float32)
        total = total.astype(jnp.bfloat16)
        thin[d] = total
        full[d, me_n] = total
        for step in range(1, narrows):
            full_copy(d, step).start()

    def finish(d):
        for step in range(1, narrows):
            full_copy(d, step).wait()
        real = full[d, 0:across].astype(jnp.float32).reshape(rows, count).astype(jnp.bfloat16)
        imag = full[d, across:narrows].astype(jnp.float32).reshape(rows, count).astype(jnp.bfloat16)
        per_r = per_all[:, 0].reshape(count, per_all.shape[3])
        per_i = per_all[:, 1].reshape(count, per_all.shape[3])

        def times(x, y):
            return jnp.dot(x, y, preferred_element_type=jnp.float32)

        prods[d, 0] = times(real, per_r) - times(imag, per_i)
        prods[d, 1] = times(real, per_i) + times(imag, per_r)

    every = range(planes)
    forward(2, every)
    for c in range(2):
        multiply(c, 0, count)
        balance(2, c)
    second_copy.wait()
    forward(1, every[:1])
    push(2, 0)
    push(2, 1)
    forward(1, every[1:])
    for c in range(2):
        multiply(c, 0, count)
        balance(1, c)
    forward(0, every[:-1])
    push(1, 0)
    push(1, 1)
    for piece in range(pieces):
        halo_copies[piece].wait()
        forward(0, every[-1:], piece * depth, (piece + 1) * depth)
        if piece == pieces // 2 - 1:
            row_done(2)
            multiply(0, 0, mid)
            multiply(1, 0, mid)
    for c in range(2):
        multiply(c, mid, count)
        balance(0, c)
    row_done(1)
    push(0, 0)
    push(0, 1)
    total_done(2)
    for one in per_copies:
        one.wait()
    total_done(1)
    finish(2)
    finish(1)
    total_done(0)
    finish(0)
    for slot in range(3):
        d = dirs[slot]
        elem_out[slot] = full[d].astype(jnp.float32).reshape(2, rows, count)
        prod_out[slot] = prods[d]


def on_device(vectors, links, directions, peram):
    count, _, _, planes, lanes = vectors.shape
    wides = lax.axis_size("wide")
    narrows = lax.axis_size("narrow")
    slots = directions.shape[0]
    cols = peram.shape[2]
    rows = count // wides
    share = 2 * rows // narrows
    across = narrows // 2
    norm = 1.0 / math.sqrt(12.0 * planes * wides * lanes * narrows)
    turned = vectors.transpose(3, 1, 2, 0, 4).reshape(planes, 6, count, lanes)
    vmem = pl.BlockSpec(memory_space=pltpu.VMEM)
    low = jnp.bfloat16
    dma = pltpu.SemaphoreType.DMA
    return pl.pallas_call(
        functools.partial(kernel, wides, narrows, norm),
        out_shape=(
            jax.ShapeDtypeStruct((slots, 2, rows, count), jnp.float32),
            jax.ShapeDtypeStruct((slots, 2, rows, cols), jnp.float32),
        ),
        in_specs=[vmem, vmem, pl.BlockSpec(memory_space=pltpu.SMEM), vmem],
        out_specs=(vmem, vmem),
        scratch_shapes=[
            pltpu.VMEM((planes, 6, count * LZ // lanes, lanes), low),
            pltpu.VMEM((6, count, lanes), low),
            pltpu.VMEM((planes, 6, count * LZ // lanes, lanes), low),
            pltpu.VMEM((count, planes * 6 * lanes), low),
            pltpu.VMEM((count, planes * 6 * lanes), low),
            pltpu.VMEM((2, count, count), jnp.float32),
            pltpu.VMEM((3, 2, across, wides, share, count), jnp.float32),
            pltpu.VMEM((3, across, wides, share, count), low),
            pltpu.VMEM((3, across, wides, share, count), jnp.float32),
            pltpu.VMEM((2, across - 1, wides, share, count), low),
            pltpu.VMEM((2, wides - 1, share, count), low),
            pltpu.VMEM((across, wides, share, count), low),
            pltpu.VMEM((3, share, count), low),
            pltpu.VMEM((3, narrows, share, count), low),
            pltpu.VMEM((3, 2, rows, cols), jnp.float32),
            pltpu.VMEM((wides, 2, rows, cols), low),
            dma((PIECES,)), dma((PIECES,)),
            dma((1,)), dma((1,)),
            dma((wides - 1,)), dma((wides - 1,)),
            dma((3, 2)), dma((3, 2)),
            dma((2, across - 1)), dma((2, across - 1)),
            dma((2, wides - 1)), dma((2, wides - 1)),
            dma((across, wides)), dma((across, wides)),
            dma((3, narrows - 1)), dma((3, narrows - 1)),
        ],
        compiler_params=pltpu.CompilerParams(
            collective_id=0, has_side_effects=True, vmem_limit_bytes=50 * 2**20),
    )(turned, links, directions, peram)


def solution(mesh):
    placed = (
        P("grp", None, None, "wide", "narrow"),
        P("grp", None, None, None, "wide", "narrow"),
        P(),
        P("grp", "wide", "narrow"),
    )
    return jax.shard_map(
        on_device,
        mesh=mesh,
        in_specs=placed,
        out_specs=(P("grp", None, "wide", None), P("grp", None, "wide", "narrow")),
        check_vma=False,
    )
```

```python
import functools
import math

import jax
import jax.numpy as jnp
from jax import lax
from jax.experimental import pallas as pl
from jax.experimental.pallas import tpu as pltpu
from jax.sharding import PartitionSpec as P

LZ = 16
ORDER = (2, 1, 0)
CHUNK = 32
MESH = pl.DeviceIdType.MESH
NT = (((1,), (1,)), ((), ()))


def kernel(wides, narrows, norm, vec, links, dirs, peram, elem_out, prod_out,
           pack, halo0, halo1, f_re, f_im, half, keep, part, got_core, got_row, got_wide,
           thin, full, prods, per_all,
           h_send, h_recv, p_send, p_recv, c_send, c_recv, r_send, r_recv,
           w_send, w_recv, g_send, g_recv):
    planes, comps, count, lanes = vec.shape
    groups = lanes // LZ
    per_group = count // groups
    rows = count // wides
    share = 2 * rows // narrows
    across = narrows // 2
    me_w = lax.axis_index("wide")
    me_n = lax.axis_index("narrow")
    core = lax.rem(me_n, 2)
    me_x = me_n // 2

    def at_wide(step):
        return {"wide": lax.rem(me_w + step, wides)}

    def at_narrow(step):
        return {"narrow": lax.rem(me_n + step, narrows)}

    def at_row(step):
        return {"narrow": lax.rem(me_x + step, across) * 2 + core}

    def copy(src, dst, send, recv, where):
        return pltpu.make_async_remote_copy(
            src_ref=src, dst_ref=dst, send_sem=send, recv_sem=recv,
            device_id=where, device_id_type=MESH)

    barrier = pltpu.get_barrier_semaphore()
    for step in range(1, wides):
        pl.semaphore_signal(barrier, inc=1, device_id=at_wide(step), device_id_type=MESH)
    for step in range(1, narrows):
        pl.semaphore_signal(barrier, inc=1, device_id=at_narrow(step), device_id_type=MESH)

    lane = lax.broadcasted_iota(jnp.int32, (CHUNK, lanes), 1)

    def pack_rows(i, carry):
        slab = i // (per_group // CHUNK)
        start = pl.multiple_of(lax.rem(i, per_group // CHUNK) * CHUNK, CHUNK)
        plane = slab // comps
        comp = lax.rem(slab, comps)
        total = jnp.zeros((CHUNK, lanes), jnp.float32)
        for group in range(groups):
            piece = vec[plane, comp, pl.ds(group * per_group + start, CHUNK), :].astype(jnp.float32)
            if group:
                piece = pltpu.roll(piece, group * LZ, 1)
            total = jnp.where(lane // LZ == group, piece, total)
        pack[plane, comp, pl.ds(start, CHUNK), :] = total.astype(jnp.bfloat16)
        return carry

    lax.fori_loop(0, planes * comps * (per_group // CHUNK), pack_rows, 0)

    pl.semaphore_wait(barrier, wides + narrows - 2)
    first_copy = copy(vec.at[0], halo0, h_send.at[0], h_recv.at[0], at_wide(wides - 1))
    second_copy = copy(pack, halo1, h_send.at[1], h_recv.at[1], at_narrow(narrows - 1))
    second_copy.start()
    first_copy.start()
    per_copies = [
        copy(peram, per_all.at[me_w], p_send.at[step - 1], p_recv.at[step - 1], at_wide(step))
        for step in range(1, wides)
    ]
    for one in per_copies:
        one.start()
    per_all[me_w] = peram[...]

    def shifted(direction, plane, comp, start):
        here = pl.ds(start, CHUNK)
        if direction == 0:
            if plane + 1 < planes:
                return vec[plane + 1, comp, here, :].astype(jnp.float32)
            return halo0[comp, here, :].astype(jnp.float32)
        own = vec[plane, comp, here, :].astype(jnp.float32)
        if direction == 1:
            group = start // per_group
            inside = pl.multiple_of(lax.rem(start, per_group), CHUNK)
            ahead = halo1[plane, comp, pl.ds(inside, CHUNK), :].astype(jnp.float32)
            ahead = pltpu.roll(ahead, lanes - LZ - LZ * group, 1)
            return jnp.where(lane < lanes - LZ, pltpu.roll(own, lanes - LZ, 1), ahead)
        return jnp.where(
            lax.rem(lane, LZ) < LZ - 1, pltpu.roll(own, lanes - 1, 1), pltpu.roll(own, LZ - 1, 1))

    def forward(direction):
        for plane in range(planes):
            def chunk(i, carry):
                start = pl.multiple_of(i * CHUNK, CHUNK)
                values = [shifted(direction, plane, comp, start) for comp in range(comps)]
                for a in range(3):
                    real = imag = None
                    for b in range(3):
                        link_r = links[direction, 0, a, b, plane:plane + 1, :]
                        link_i = links[direction, 1, a, b, plane:plane + 1, :]
                        term_r = link_r * values[b] - link_i * values[3 + b]
                        term_i = link_r * values[3 + b] + link_i * values[b]
                        real = term_r if real is None else real + term_r
                        imag = term_i if imag is None else imag + term_i
                    real = real.astype(jnp.bfloat16)
                    imag = imag.astype(jnp.bfloat16)
                    low = (plane * comps + a) * lanes
                    high = low + 3 * lanes
                    f_re[pl.ds(start, CHUNK), low:low + lanes] = real
                    f_re[pl.ds(start, CHUNK), high:high + lanes] = imag
                    f_im[pl.ds(start, CHUNK), low:low + lanes] = imag
                    f_im[pl.ds(start, CHUNK), high:high + lanes] = -real
                return carry

            lax.fori_loop(0, count // CHUNK, chunk, 0)

    def compute(direction):
        forward(direction)
        left = jnp.concatenate(
            [vec[plane, comp] for plane in range(planes) for comp in range(comps)], 1)
        half[0] = lax.dot_general(left, f_re[...], NT, preferred_element_type=jnp.float32)
        half[1] = lax.dot_general(left, f_im[...], NT, preferred_element_type=jnp.float32)
        block = lanes
        for c in range(2):
            for top in range(0, count, block):
                turned = half[c, :, top:top + block].T
                own = half[c, top:top + block, :]
                terms = ((own - turned) if c == 0 else (own + turned)) * norm
                for low in range(0, block, share):
                    row = top + low
                    owner = c * across + (row % rows) // share
                    piece = terms[low:low + share]
                    keep[direction, owner % 2, owner // 2, row // rows] = piece
                    part[direction, owner % 2, owner // 2, row // rows] = piece.astype(jnp.bfloat16)

    def core_copy(d):
        return copy(part.at[d, 1 - core], got_core.at[d], c_send.at[d], c_recv.at[d],
                    {"narrow": me_x * 2 + 1 - core})

    def row_copy(d, step):
        return copy(part.at[d, core, lax.rem(me_x + step, across)], got_row.at[d, step - 1],
                    r_send.at[d, step - 1], r_recv.at[d, step - 1], at_row(step))

    def wide_copy(d, step):
        return copy(part.at[d, core, me_x, lax.rem(me_w + step, wides)],
                    got_wide.at[d, step - 1],
                    w_send.at[d, step - 1], w_recv.at[d, step - 1], at_wide(step))

    def full_copy(d, step):
        return copy(thin.at[d], full.at[d, me_n], g_send.at[d, step - 1], g_recv.at[d, step - 1],
                    at_narrow(step))

    def core_done(d):
        core_copy(d).wait()
        for x in range(across):
            def add(w, carry):
                total = keep[d, core, x, w] + got_core[d, x, w].astype(jnp.float32)
                keep[d, core, x, w] = total
                part[d, core, x, w] = total.astype(jnp.bfloat16)
                return carry
            lax.fori_loop(0, wides, add, 0)
        for step in range(1, across):
            row_copy(d, step).start()

    def row_done(d):
        for step in range(1, across):
            row_copy(d, step).wait()

        def add(w, carry):
            total = keep[d, core, me_x, w]
            for step in range(1, across):
                total = total + got_row[d, step - 1, w].astype(jnp.float32)
            keep[d, core, me_x, w] = total
            part[d, core, me_x, w] = total.astype(jnp.bfloat16)
            return carry

        lax.fori_loop(0, wides, add, 0)
        for step in range(1, wides):
            wide_copy(d, step).start()

    def wide_done(d):
        for step in range(1, wides):
            wide_copy(d, step).wait()
        total = keep[d, core, me_x, me_w]
        for step in range(1, wides):
            total = total + got_wide[d, step - 1].astype(jnp.float32)
        total = total.astype(jnp.bfloat16)
        thin[d] = total
        full[d, me_n] = total
        for step in range(1, narrows):
            full_copy(d, step).start()

    def finish(d):
        for step in range(1, narrows):
            full_copy(d, step).wait()
        real = full[d, 0:across].astype(jnp.float32).reshape(rows, count).astype(jnp.bfloat16)
        imag = full[d, across:narrows].astype(jnp.float32).reshape(rows, count).astype(jnp.bfloat16)
        per_r = per_all[:, 0].reshape(count, per_all.shape[3])
        per_i = per_all[:, 1].reshape(count, per_all.shape[3])

        def times(x, y):
            return jnp.dot(x, y, preferred_element_type=jnp.float32)

        prods[d, 0] = times(real, per_r) - times(imag, per_i)
        prods[d, 1] = times(real, per_i) + times(imag, per_r)

    compute(2)
    core_copy(2).start()
    second_copy.wait()
    compute(1)
    core_copy(1).start()
    core_done(2)
    first_copy.wait()
    compute(0)
    core_copy(0).start()
    row_done(2)
    core_done(1)
    core_done(0)
    row_done(1)
    wide_done(2)
    row_done(0)
    for one in per_copies:
        one.wait()
    wide_done(1)
    finish(2)
    wide_done(0)
    finish(1)
    finish(0)
    for slot in range(3):
        d = dirs[slot]
        elem_out[slot] = full[d].astype(jnp.float32).reshape(2, rows, count)
        prod_out[slot] = prods[d]


def on_device(vectors, links, directions, peram):
    count, _, _, planes, lanes = vectors.shape
    wides = lax.axis_size("wide")
    narrows = lax.axis_size("narrow")
    slots = directions.shape[0]
    cols = peram.shape[2]
    rows = count // wides
    share = 2 * rows // narrows
    across = narrows // 2
    norm = 1.0 / math.sqrt(12.0 * planes * wides * lanes * narrows)
    turned = vectors.transpose(3, 1, 2, 0, 4).reshape(planes, 6, count, lanes)
    vmem = pl.BlockSpec(memory_space=pltpu.VMEM)
    low = jnp.bfloat16
    dma = pltpu.SemaphoreType.DMA
    return pl.pallas_call(
        functools.partial(kernel, wides, narrows, norm),
        out_shape=(
            jax.ShapeDtypeStruct((slots, 2, rows, count), jnp.float32),
            jax.ShapeDtypeStruct((slots, 2, rows, cols), jnp.float32),
        ),
        in_specs=[vmem, vmem, pl.BlockSpec(memory_space=pltpu.SMEM), vmem],
        out_specs=(vmem, vmem),
        scratch_shapes=[
            pltpu.VMEM((planes, 6, count * LZ // lanes, lanes), low),
            pltpu.VMEM((6, count, lanes), low),
            pltpu.VMEM((planes, 6, count * LZ // lanes, lanes), low),
            pltpu.VMEM((count, planes * 6 * lanes), low),
            pltpu.VMEM((count, planes * 6 * lanes), low),
            pltpu.VMEM((2, count, count), jnp.float32),
            pltpu.VMEM((3, 2, across, wides, share, count), jnp.float32),
            pltpu.VMEM((3, 2, across, wides, share, count), low),
            pltpu.VMEM((3, across, wides, share, count), low),
            pltpu.VMEM((3, across - 1, wides, share, count), low),
            pltpu.VMEM((3, wides - 1, share, count), low),
            pltpu.VMEM((3, share, count), low),
            pltpu.VMEM((3, narrows, share, count), low),
            pltpu.VMEM((3, 2, rows, cols), jnp.float32),
            pltpu.VMEM((wides, 2, rows, cols), low),
            dma((2,)), dma((2,)),
            dma((wides - 1,)), dma((wides - 1,)),
            dma((3,)), dma((3,)),
            dma((3, across - 1)), dma((3, across - 1)),
            dma((3, wides - 1)), dma((3, wides - 1)),
            dma((3, narrows - 1)), dma((3, narrows - 1)),
        ],
        compiler_params=pltpu.CompilerParams(
            collective_id=0, has_side_effects=True, vmem_limit_bytes=50 * 2**20),
    )(turned, links, directions, peram)


def solution(mesh):
    placed = (
        P("grp", None, None, "wide", "narrow"),
        P("grp", None, None, None, "wide", "narrow"),
        P(),
        P("grp", "wide", "narrow"),
    )
    return jax.shard_map(
        on_device,
        mesh=mesh,
        in_specs=placed,
        out_specs=(P("grp", None, "wide", None), P("grp", None, "wide", "narrow")),
        check_vma=False,
    )
```

```python
import functools
import math

import jax
import jax.numpy as jnp
from jax import lax
from jax.experimental import pallas as pl
from jax.experimental.pallas import tpu as pltpu
from jax.sharding import PartitionSpec as P

LZ = 16
ORDER = (2, 1, 0)
CHUNK = 32
MESH = pl.DeviceIdType.MESH
NT = (((1,), (1,)), ((), ()))


def kernel(wides, narrows, norm, vec, links, dirs, peram, elem_out, prod_out,
           pack, halo0, halo1, f_re, f_im, half, keep, part, got_core, got_row, got_wide,
           thin, full, prods, per_all,
           h_send, h_recv, p_send, p_recv, c_send, c_recv, r_send, r_recv,
           w_send, w_recv, g_send, g_recv):
    planes, comps, count, lanes = vec.shape
    groups = lanes // LZ
    per_group = count // groups
    rows = count // wides
    share = 2 * rows // narrows
    across = narrows // 2
    me_w = lax.axis_index("wide")
    me_n = lax.axis_index("narrow")
    core = lax.rem(me_n, 2)
    me_x = me_n // 2

    def at_wide(step):
        return {"wide": lax.rem(me_w + step, wides)}

    def at_narrow(step):
        return {"narrow": lax.rem(me_n + step, narrows)}

    def at_row(step):
        return {"narrow": lax.rem(me_x + step, across) * 2 + core}

    def copy(src, dst, send, recv, where):
        return pltpu.make_async_remote_copy(
            src_ref=src, dst_ref=dst, send_sem=send, recv_sem=recv,
            device_id=where, device_id_type=MESH)

    barrier = pltpu.get_barrier_semaphore()
    for step in range(1, wides):
        pl.semaphore_signal(barrier, inc=1, device_id=at_wide(step), device_id_type=MESH)
    for step in range(1, narrows):
        pl.semaphore_signal(barrier, inc=1, device_id=at_narrow(step), device_id_type=MESH)

    lane = lax.broadcasted_iota(jnp.int32, (CHUNK, lanes), 1)

    def pack_rows(i, carry):
        slab = i // (per_group // CHUNK)
        start = pl.multiple_of(lax.rem(i, per_group // CHUNK) * CHUNK, CHUNK)
        plane = slab // comps
        comp = lax.rem(slab, comps)
        total = jnp.zeros((CHUNK, lanes), jnp.float32)
        for group in range(groups):
            piece = vec[plane, comp, pl.ds(group * per_group + start, CHUNK), :].astype(jnp.float32)
            if group:
                piece = pltpu.roll(piece, group * LZ, 1)
            total = jnp.where(lane // LZ == group, piece, total)
        pack[plane, comp, pl.ds(start, CHUNK), :] = total.astype(jnp.bfloat16)
        return carry

    pl.semaphore_wait(barrier, wides + narrows - 2)
    first_copy = copy(vec.at[0], halo0, h_send.at[0], h_recv.at[0], at_wide(wides - 1))
    second_copy = copy(pack, halo1, h_send.at[1], h_recv.at[1], at_narrow(narrows - 1))
    first_copy.start()
    lax.fori_loop(0, planes * comps * (per_group // CHUNK), pack_rows, 0)
    second_copy.start()
    per_copies = [
        copy(peram, per_all.at[me_w], p_send.at[step - 1], p_recv.at[step - 1], at_wide(step))
        for step in range(1, wides)
    ]
    for one in per_copies:
        one.start()
    per_all[me_w] = peram[...]

    def shifted(direction, plane, comp, start):
        here = pl.ds(start, CHUNK)
        if direction == 0:
            if plane + 1 < planes:
                return vec[plane + 1, comp, here, :].astype(jnp.float32)
            return halo0[comp, here, :].astype(jnp.float32)
        own = vec[plane, comp, here, :].astype(jnp.float32)
        if direction == 1:
            group = start // per_group
            inside = pl.multiple_of(lax.rem(start, per_group), CHUNK)
            ahead = halo1[plane, comp, pl.ds(inside, CHUNK), :].astype(jnp.float32)
            ahead = pltpu.roll(ahead, lanes - LZ - LZ * group, 1)
            return jnp.where(lane < lanes - LZ, pltpu.roll(own, lanes - LZ, 1), ahead)
        return jnp.where(
            lax.rem(lane, LZ) < LZ - 1, pltpu.roll(own, lanes - 1, 1), pltpu.roll(own, LZ - 1, 1))

    def forward(direction, planes_here=None):
        for plane in planes_here or range(planes):
            def chunk(i, carry):
                start = pl.multiple_of(i * CHUNK, CHUNK)
                values = [shifted(direction, plane, comp, start) for comp in range(comps)]
                for a in range(3):
                    real = imag = None
                    for b in range(3):
                        link_r = links[direction, 0, a, b, plane:plane + 1, :]
                        link_i = links[direction, 1, a, b, plane:plane + 1, :]
                        term_r = link_r * values[b] - link_i * values[3 + b]
                        term_i = link_r * values[3 + b] + link_i * values[b]
                        real = term_r if real is None else real + term_r
                        imag = term_i if imag is None else imag + term_i
                    real = real.astype(jnp.bfloat16)
                    imag = imag.astype(jnp.bfloat16)
                    low = (plane * comps + a) * lanes
                    high = low + 3 * lanes
                    f_re[pl.ds(start, CHUNK), low:low + lanes] = real
                    f_re[pl.ds(start, CHUNK), high:high + lanes] = imag
                    f_im[pl.ds(start, CHUNK), low:low + lanes] = imag
                    f_im[pl.ds(start, CHUNK), high:high + lanes] = -real
                return carry

            lax.fori_loop(0, count // CHUNK, chunk, 0)

    def compute(direction):
        left = jnp.concatenate(
            [vec[plane, comp] for plane in range(planes) for comp in range(comps)], 1)
        half[0] = lax.dot_general(left, f_re[...], NT, preferred_element_type=jnp.float32)
        half[1] = lax.dot_general(left, f_im[...], NT, preferred_element_type=jnp.float32)
        block = lanes
        for c in range(2):
            for top in range(0, count, block):
                turned = half[c, :, top:top + block].T
                own = half[c, top:top + block, :]
                terms = ((own - turned) if c == 0 else (own + turned)) * norm
                for low in range(0, block, share):
                    row = top + low
                    owner = c * across + (row % rows) // share
                    piece = terms[low:low + share]
                    keep[direction, owner % 2, owner // 2, row // rows] = piece
                    part[direction, owner % 2, owner // 2, row // rows] = piece.astype(jnp.bfloat16)

    def core_copy(d):
        return copy(part.at[d, 1 - core], got_core.at[d], c_send.at[d], c_recv.at[d],
                    {"narrow": me_x * 2 + 1 - core})

    def row_copy(d, step):
        return copy(part.at[d, core, lax.rem(me_x + step, across)], got_row.at[d, step - 1],
                    r_send.at[d, step - 1], r_recv.at[d, step - 1], at_row(step))

    def wide_copy(d, step):
        return copy(part.at[d, core, me_x, lax.rem(me_w + step, wides)],
                    got_wide.at[d, step - 1],
                    w_send.at[d, step - 1], w_recv.at[d, step - 1], at_wide(step))

    def full_copy(d, step):
        return copy(thin.at[d], full.at[d, me_n], g_send.at[d, step - 1], g_recv.at[d, step - 1],
                    at_narrow(step))

    def core_done(d):
        core_copy(d).wait()
        for x in range(across):
            def add(w, carry):
                total = keep[d, core, x, w] + got_core[d, x, w].astype(jnp.float32)
                keep[d, core, x, w] = total
                part[d, core, x, w] = total.astype(jnp.bfloat16)
                return carry
            lax.fori_loop(0, wides, add, 0)
        for step in range(1, across):
            row_copy(d, step).start()

    def row_done(d):
        for step in range(1, across):
            row_copy(d, step).wait()

        def add(w, carry):
            total = keep[d, core, me_x, w]
            for step in range(1, across):
                total = total + got_row[d, step - 1, w].astype(jnp.float32)
            keep[d, core, me_x, w] = total
            part[d, core, me_x, w] = total.astype(jnp.bfloat16)
            return carry

        lax.fori_loop(0, wides, add, 0)
        for step in range(1, wides):
            wide_copy(d, step).start()

    def wide_done(d):
        for step in range(1, wides):
            wide_copy(d, step).wait()
        total = keep[d, core, me_x, me_w]
        for step in range(1, wides):
            total = total + got_wide[d, step - 1].astype(jnp.float32)
        total = total.astype(jnp.bfloat16)
        thin[d] = total
        full[d, me_n] = total
        for step in range(1, narrows):
            full_copy(d, step).start()

    def finish(d):
        for step in range(1, narrows):
            full_copy(d, step).wait()
        real = full[d, 0:across].astype(jnp.float32).reshape(rows, count).astype(jnp.bfloat16)
        imag = full[d, across:narrows].astype(jnp.float32).reshape(rows, count).astype(jnp.bfloat16)
        per_r = per_all[:, 0].reshape(count, per_all.shape[3])
        per_i = per_all[:, 1].reshape(count, per_all.shape[3])

        def times(x, y):
            return jnp.dot(x, y, preferred_element_type=jnp.float32)

        prods[d, 0] = times(real, per_r) - times(imag, per_i)
        prods[d, 1] = times(real, per_i) + times(imag, per_r)

    forward(2)
    compute(2)
    core_copy(2).start()
    second_copy.wait()
    forward(1)
    core_done(2)
    compute(1)
    core_copy(1).start()
    forward(0, range(planes - 1))
    core_done(1)
    row_done(2)
    first_copy.wait()
    forward(0, range(planes - 1, planes))
    compute(0)
    core_copy(0).start()
    core_done(0)
    row_done(1)
    wide_done(2)
    row_done(0)
    for one in per_copies:
        one.wait()
    wide_done(1)
    finish(2)
    wide_done(0)
    finish(1)
    finish(0)
    for slot in range(3):
        d = dirs[slot]
        elem_out[slot] = full[d].astype(jnp.float32).reshape(2, rows, count)
        prod_out[slot] = prods[d]


def on_device(vectors, links, directions, peram):
    count, _, _, planes, lanes = vectors.shape
    wides = lax.axis_size("wide")
    narrows = lax.axis_size("narrow")
    slots = directions.shape[0]
    cols = peram.shape[2]
    rows = count // wides
    share = 2 * rows // narrows
    across = narrows // 2
    norm = 1.0 / math.sqrt(12.0 * planes * wides * lanes * narrows)
    turned = vectors.transpose(3, 1, 2, 0, 4).reshape(planes, 6, count, lanes)
    vmem = pl.BlockSpec(memory_space=pltpu.VMEM)
    low = jnp.bfloat16
    dma = pltpu.SemaphoreType.DMA
    return pl.pallas_call(
        functools.partial(kernel, wides, narrows, norm),
        out_shape=(
            jax.ShapeDtypeStruct((slots, 2, rows, count), jnp.float32),
            jax.ShapeDtypeStruct((slots, 2, rows, cols), jnp.float32),
        ),
        in_specs=[vmem, vmem, pl.BlockSpec(memory_space=pltpu.SMEM), vmem],
        out_specs=(vmem, vmem),
        scratch_shapes=[
            pltpu.VMEM((planes, 6, count * LZ // lanes, lanes), low),
            pltpu.VMEM((6, count, lanes), low),
            pltpu.VMEM((planes, 6, count * LZ // lanes, lanes), low),
            pltpu.VMEM((count, planes * 6 * lanes), low),
            pltpu.VMEM((count, planes * 6 * lanes), low),
            pltpu.VMEM((2, count, count), jnp.float32),
            pltpu.VMEM((3, 2, across, wides, share, count), jnp.float32),
            pltpu.VMEM((3, 2, across, wides, share, count), low),
            pltpu.VMEM((3, across, wides, share, count), low),
            pltpu.VMEM((3, across - 1, wides, share, count), low),
            pltpu.VMEM((3, wides - 1, share, count), low),
            pltpu.VMEM((3, share, count), low),
            pltpu.VMEM((3, narrows, share, count), low),
            pltpu.VMEM((3, 2, rows, cols), jnp.float32),
            pltpu.VMEM((wides, 2, rows, cols), low),
            dma((2,)), dma((2,)),
            dma((wides - 1,)), dma((wides - 1,)),
            dma((3,)), dma((3,)),
            dma((3, across - 1)), dma((3, across - 1)),
            dma((3, wides - 1)), dma((3, wides - 1)),
            dma((3, narrows - 1)), dma((3, narrows - 1)),
        ],
        compiler_params=pltpu.CompilerParams(
            collective_id=0, has_side_effects=True, vmem_limit_bytes=50 * 2**20),
    )(turned, links, directions, peram)


def solution(mesh):
    placed = (
        P("grp", None, None, "wide", "narrow"),
        P("grp", None, None, None, "wide", "narrow"),
        P(),
        P("grp", "wide", "narrow"),
    )
    return jax.shard_map(
        on_device,
        mesh=mesh,
        in_specs=placed,
        out_specs=(P("grp", None, "wide", None), P("grp", None, "wide", "narrow")),
        check_vma=False,
    )
```
